128 devices in a mesh: layer: 16 (over z_lo, x, core), lat: 8 (over z_hi, y).
Axes of the slice: x: 4, y: 4, z: 4 (z_hi: 2, z_lo: 2; z = z_hi * 2 + z_lo), core: 2. Of those that a mesh axis runs over, the one named last changes fastest.
Arguments:
- saved_codes: bfloat16 [16, 512, 1024], P('layer', 'lat'), may hold values from 0.049804688 to 2
- relu_mask: int32 [16, 512, 1024], P('layer', 'lat'), may hold values 0 or 1
- errors: bfloat16 [16, 1024, 4096], P('layer'), may hold values from -0.29882812 to 0.29882812
- decoders: bfloat16 [16, 16, 512, 4096], P('layer', None, 'lat'), may hold values from -0.59765625 to 0.59765625
- inputs: bfloat16 [16, 1024, 4096], P('layer'), may hold values from -0.3984375 to 0.3984375
Outputs:
- decoder_grad: bfloat16 [16, 16, 512, 4096], P('layer', None, 'lat')
- code_grad: float32 [16, 512, 1024], P('layer', 'lat')
- encoder_grad: bfloat16 [16, 512, 4096], P('layer', 'lat')
The draws below stay inside these ranges and needn't reach their ends.
All inputs are finite; a program needn't handle non-finite values. No bound on the sum of `relu_mask` on one device may be relied on, other than what follows from the above.
Results may differ from the reference program's by a relative error of at most 0.0049.
Values may be sent and summed in bfloat16 or wider, within the bound.
No kernel may reach another device: no remote copies, remote signals or barrier semaphores. Data moves between devices by JAX's collectives and lax.ppermute only.
A program may use at most 128 MiB of HBM per device.

```python
import math
import jax
import jax.numpy as jnp
from jax import lax

D = 4096
LATENTS = 512
TOKENS = 1024
LAYERS = 16


def touch_ends(array, own_key, low, largest):
    shape = array.shape
    spot = [jax.random.randint(jax.random.fold_in(own_key, axis), (), 0, shape[axis]) for axis in range(len(shape))]
    array = array.at[tuple(spot)].set(low)
    longest = shape.index(max(shape))
    spot[longest] = (spot[longest] + 1) % shape[longest]
    return array.at[tuple(spot)].set(largest)


def spiked(result, own_key, source, target, parts, factor):
    owner, partner = [(jnp.arange(result.shape[position]) // (result.shape[position] // parts)).reshape([-1 if axis == position else 1 for axis in range(result.ndim)]) for position in (source, target)]
    chosen = jax.random.permutation(own_key, parts)[partner]
    strong = (owner == chosen) | (owner == (partner + parts // 2) % parts)
    return jnp.where(strong, factor * result, result)


def steps_of(own_key, shape, shards, least, largest):
    factor_of = 1.0
    for dim, parts in shards:
        draws = jax.random.uniform(jax.random.fold_in(jax.random.fold_in(own_key, 6), dim), (parts,), jnp.float32, least / len(shards), largest / len(shards))
        factor_of = factor_of * jnp.repeat(jnp.exp(draws), shape[dim] // parts).reshape((-1,) + (1,) * (len(shape) - 1 - dim))
    return factor_of


def scatter_about(own_key, dims, spread, limit, pieces=(), held_as=jnp.bfloat16):
    level = steps_of(own_key, dims, pieces, -0.22, 0.18) if pieces else 1.0
    result = jax.random.normal(own_key, dims, jnp.float32) * spread * level
    return jnp.minimum(jnp.maximum(result, -limit), limit).astype(held_as)


def gaussian_with(stream_key, shape, deviation, limit, shards, heavy, held_as=jnp.bfloat16):
    entries = deviation * jax.random.normal(stream_key, shape, jnp.float32)
    if shards:
        entries = entries * steps_of(stream_key, shape, shards, -0.22, 0.18)
    return jnp.clip(spiked(entries, jax.random.fold_in(stream_key, 3), *heavy), -limit, limit).astype(held_as)


def setup_inputs(seed: int = 0) -> dict:
    splits = jax.random.split(jax.random.key(seed), 6)
    saved_codes = jnp.clip(jnp.exp(math.log(2.0) - 3.6927934 * jax.random.uniform(splits[0], (LAYERS, LATENTS, TOKENS), jnp.float32) ** steps_of(splits[0], (LAYERS, LATENTS, TOKENS), ((0, 16), (1, 8)), -0.2, 0.2)), 0.049804688, 2.0).astype(jnp.bfloat16)
    relu_mask = touch_ends((jax.random.randint(splits[1], (LAYERS, LATENTS, TOKENS), 0, 2) < 1).astype(jnp.int32), jax.random.fold_in(splits[1], 1), 0, 1)
    errors = scatter_about(splits[2], (LAYERS, TOKENS, D), 0.05, 0.29882812, ((0, 16),))
    decoders = gaussian_with(splits[3], (LAYERS, LAYERS, LATENTS, D), 0.1, 0.59765625, ((0, 16), (2, 8)), (0, 1, 16, 2.0))
    inputs = scatter_about(splits[4], (LAYERS, TOKENS, D), 0.0625, 0.3984375, ((0, 16),))
    return {"saved_codes": saved_codes, "relu_mask": relu_mask, "errors": errors, "decoders": decoders, "inputs": inputs}


def reference(saved_codes, relu_mask, errors, decoders, inputs):
    active = saved_codes * relu_mask.astype(jnp.bfloat16)
    flat_active = active.reshape(LAYERS * LATENTS, TOKENS)
    sources = jnp.arange(LAYERS, dtype=jnp.int32)

    def per_target(running, packed):
        target, target_error, decoder_rows = packed
        allowed = (sources <= target)[:, None, None]
        products = jnp.dot(flat_active, target_error, preferred_element_type=jnp.float32).reshape(LAYERS, LATENTS, D)
        products = jnp.where(allowed, products, 0.0).astype(jnp.bfloat16)
        terms = lax.dot_general(decoder_rows.reshape(LAYERS * LATENTS, D), target_error, (((1,), (1,)), ((), ())), preferred_element_type=jnp.float32).reshape(LAYERS, LATENTS, TOKENS)
        return running + jnp.where(allowed, terms, 0.0), products

    start_sum = jnp.zeros((LAYERS, LATENTS, TOKENS), jnp.float32)
    code_grad, decoder_grad = lax.scan(per_target, start_sum, (sources, errors, decoders))
    pre_grad = (code_grad * relu_mask.astype(jnp.float32)).astype(jnp.bfloat16)
    encoder_grad = jnp.einsum("lfn,lnd->lfd", pre_grad.astype(jnp.float32), inputs.astype(jnp.float32)).astype(jnp.bfloat16)
    return decoder_grad, code_grad, encoder_grad
```

```python
import jax
import jax.numpy as jnp
from jax import lax
from jax.sharding import PartitionSpec as P

CORES = 2


def body(saved_codes, relu_mask, errors, decoders, inputs):
    layers = lax.axis_size("layer")
    chips = layers // CORES
    target = lax.axis_index("layer")
    core = target % CORES
    chip = target // CORES
    latents, tokens = saved_codes.shape[1:]
    target_error = errors[0]
    width = target_error.shape[1]
    same_core = [[chip_ * CORES + c for chip_ in range(chips)] for c in range(CORES)]
    swap = [(i, i ^ 1) for i in range(layers)]
    chip_ids = jnp.arange(chips, dtype=jnp.int32)

    active = saved_codes * relu_mask.astype(jnp.bfloat16)
    copies = jnp.broadcast_to(active, (chips, latents, tokens))
    mine = lax.all_to_all(copies, "layer", 0, 0, tiled=True, axis_index_groups=same_core)

    slabs = decoders[0].reshape(chips, CORES, latents, width)
    allowed_mine = chip_ids <= chip
    allowed_other = (chip_ids * CORES + (1 - core)) <= target

    def terms(c, allowed):
        rows = lax.dynamic_index_in_dim(slabs, c, 1, keepdims=False).reshape(chips * latents, width)
        products = lax.dot_general(
            rows, target_error, (((1,), (1,)), ((), ())), preferred_element_type=jnp.float32
        ).reshape(chips, latents, tokens)
        return jnp.where(allowed[:, None, None], products, 0.0)

    away = lax.ppermute(terms(1 - core, allowed_other), "layer", swap)
    pair = (terms(core, allowed_mine) + away).astype(jnp.bfloat16)
    back = lax.all_to_all(pair, "layer", 0, 0, tiled=True, axis_index_groups=same_core)

    other = lax.ppermute(mine, "layer", swap)

    def grads(rows, allowed):
        products = jnp.dot(
            rows.reshape(chips * latents, tokens), target_error, preferred_element_type=jnp.float32
        ).reshape(chips, latents, width)
        return jnp.where(allowed[:, None, None], products, 0.0).astype(jnp.bfloat16)

    own_grads = grads(mine, allowed_mine)
    other_grads = grads(other, allowed_other)
    even = core == 0
    decoder_grad = jnp.stack(
        [jnp.where(even, own_grads, other_grads), jnp.where(even, other_grads, own_grads)], axis=1
    ).reshape(1, layers, latents, width)

    code_grad = jnp.sum(back.astype(jnp.float32), axis=0)
    pre_grad = (code_grad * relu_mask[0].astype(jnp.float32)).astype(jnp.bfloat16)
    encoder_grad = jnp.dot(pre_grad, inputs[0], preferred_element_type=jnp.float32)
    return decoder_grad, code_grad[None], encoder_grad.astype(jnp.bfloat16)[None]


def solution(mesh):
    return jax.shard_map(
        body,
        mesh=mesh,
        in_specs=(
            P("layer", "lat", None),
            P("layer", "lat", None),
            P("layer", None, None),
            P("layer", None, "lat", None),
            P("layer", None, None),
        ),
        out_specs=(P("layer", None, "lat", None), P("layer", "lat", None), P("layer", "lat", None)),
        check_vma=False,
    )
```

```python
import jax
import jax.numpy as jnp
from jax import lax
from jax.experimental import pallas as pl
from jax.experimental.pallas import tpu as pltpu
from jax.sharding import PartitionSpec as P


CORES = 2
AHEAD = 3
DEPTHS = (256, 512, 1024, 1024, 1280)
COLUMNS = (512, 1024, 1024, 768, 512, 256)

HBM = pl.BlockSpec(memory_space=pltpu.HBM)
VMEM = pl.BlockSpec(memory_space=pltpu.VMEM)
SMEM = pl.BlockSpec(memory_space=pltpu.SMEM)


def params(mib):
    return pltpu.CompilerParams(vmem_limit_bytes=mib << 20)


def starts(sizes):
    return [sum(sizes[:i]) for i in range(len(sizes))]


def gate(codes, mask, chips):
    latents, tokens = codes.shape

    def kernel(codes_hbm, mask_hbm, out_hbm, buf, mask_buf, sems):
        loads = [
            pltpu.make_async_copy(codes_hbm, buf, sems.at[chips]),
            pltpu.make_async_copy(mask_hbm, mask_buf, sems.at[chips + 1]),
        ]
        copies = [
            pltpu.make_async_copy(buf, out_hbm.at[chip], sems.at[chip]) for chip in range(chips)
        ]
        for load in loads:
            load.start()
        for load in loads:
            load.wait()
        buf[...] = buf[...] * mask_buf[...].astype(jnp.bfloat16)
        for copy in copies:
            copy.start()
        for copy in copies:
            copy.wait()

    return pl.pallas_call(
        kernel,
        out_shape=jax.ShapeDtypeStruct((chips, latents, tokens), jnp.bfloat16),
        in_specs=[HBM, HBM],
        out_specs=HBM,
        scratch_shapes=[
            pltpu.VMEM((latents, tokens), jnp.bfloat16),
            pltpu.VMEM((latents, tokens), jnp.int32),
            pltpu.SemaphoreType.DMA((chips + 2,)),
        ],
        compiler_params=params(4),
        name="gate",
    )(codes, mask)


def code_terms(place, slabs, errors, hand_on):
    chips, _, latents, width = slabs.shape
    tokens = errors.shape[0]
    rows = chips * latents
    offsets = starts(DEPTHS)
    steps = len(DEPTHS)
    parts = 2

    def kernel(place_ref, slab_hbm, error_hbm, out, *refs):
        acc = refs[0] if hand_on else out
        slab_buf, error_buf, sems, out_sems = refs[-4:]
        parity, target = place_ref[0], place_ref[1]
        loads = []
        for k in range(steps):
            cols = pl.ds(offsets[k], DEPTHS[k])
            loads.append((
                pltpu.make_async_copy(error_hbm.at[:, cols], error_buf.at[:, cols], sems.at[0, k]),
                pltpu.make_async_copy(
                    slab_hbm.at[:, parity, :, cols], slab_buf.at[:, :, cols], sems.at[1, k]
                ),
            ))
        for pair in loads[:AHEAD]:
            for load in pair:
                load.start()
        source = (lax.broadcasted_iota(jnp.int32, (1, rows), 1) // latents) * CORES + parity
        keep = (source <= target).astype(jnp.float32)
        stores = []
        for k in range(steps):
            cols = pl.ds(offsets[k], DEPTHS[k])
            for load in loads[k]:
                load.wait()
            if k + AHEAD < steps:
                for load in loads[k + AHEAD]:
                    load.start()
            last = k == steps - 1
            count = parts if last else 1
            wide = rows // count
            for n in range(count):
                here = pl.ds(n * wide, wide)
                some = pl.ds(n * (chips // count), chips // count)
                part = lax.dot_general(
                    error_buf[:, cols], slab_buf[some, :, cols].reshape(wide, DEPTHS[k]),
                    (((1,), (1,)), ((), ())), preferred_element_type=jnp.float32,
                )
                if k == 0:
                    acc[:, here] = part
                elif not last:
                    acc[:, here] += part
                else:
                    acc[:, here] = (acc[:, here] + part) * keep[:, n * wide : (n + 1) * wide]
                    if hand_on:
                        store = pltpu.make_async_copy(
                            acc.at[:, here], out.at[:, here], out_sems.at[n]
                        )
                        store.start()
                        stores.append(store)
        for store in stores:
            store.wait()

    scratch = [
        pltpu.VMEM((chips, latents, width), jnp.bfloat16),
        pltpu.VMEM((tokens, width), jnp.bfloat16),
        pltpu.SemaphoreType.DMA((2, steps)),
        pltpu.SemaphoreType.DMA((parts,)),
    ]
    if hand_on:
        scratch = [pltpu.VMEM((tokens, rows), jnp.float32)] + scratch
    return pl.pallas_call(
        kernel,
        out_shape=jax.ShapeDtypeStruct((tokens, rows), jnp.float32),
        in_specs=[SMEM, HBM, HBM],
        out_specs=HBM if hand_on else VMEM,
        scratch_shapes=scratch,
        compiler_params=params(24),
        cost_estimate=pl.CostEstimate(
            flops=2 * rows * tokens * width, transcendentals=0,
            bytes_accessed=2 * (rows + tokens) * width,
        ),
        name="code_away" if hand_on else "code_own",
    )(place, slabs, errors)


def join(own, away, chips):
    tokens, rows = own.shape
    latents = rows // chips
    half, lanes = tokens // 2, CORES * latents
    pairs = rows // lanes

    def kernel(own_ref, away_ref, out_hbm, out_buf, sems):
        left = lax.broadcasted_iota(jnp.int32, (half, lanes), 1) < latents
        stores = []
        for pair in range(pairs):
            cols = pl.ds(pair * lanes, lanes)
            low = own_ref[pl.ds(0, half), cols] + away_ref[pl.ds(0, half), cols]
            high = own_ref[pl.ds(half, half), cols] + away_ref[pl.ds(half, half), cols]
            out_buf[2 * pair] = jnp.where(
                left, low, pltpu.roll(high, latents, axis=1)
            ).astype(jnp.bfloat16)
            out_buf[2 * pair + 1] = jnp.where(
                left, pltpu.roll(low, latents, axis=1), high
            ).astype(jnp.bfloat16)
            both = pl.ds(2 * pair, 2)
            store = pltpu.make_async_copy(out_buf.at[both], out_hbm.at[both], sems.at[pair])
            store.start()
            stores.append(store)
        for store in stores:
            store.wait()

    return pl.pallas_call(
        kernel,
        out_shape=jax.ShapeDtypeStruct((chips, half, lanes), jnp.bfloat16),
        in_specs=[VMEM, VMEM],
        out_specs=HBM,
        scratch_shapes=[
            pltpu.VMEM((chips, half, lanes), jnp.bfloat16),
            pltpu.SemaphoreType.DMA((pairs,)),
        ],
        compiler_params=params(8),
        name="join",
    )(own, away)


def decoder(place, own, other, errors):
    tokens, width = errors.shape
    chips, latents, _ = own.shape
    rows = chips * CORES * latents
    offsets = starts(COLUMNS)
    steps = len(COLUMNS)

    def kernel(place_ref, error_hbm, own_ref, other_ref, out_hbm, lhs, error_buf, out_buf, sems):
        parity, target = place_ref[0], place_ref[1]
        loads, stores = [], []
        for k in range(steps):
            cols = pl.ds(offsets[k], COLUMNS[k])
            loads.append(
                pltpu.make_async_copy(error_hbm.at[:, cols], error_buf.at[:, cols], sems.at[0, k])
            )
            stores.append(
                pltpu.make_async_copy(out_buf.at[:, cols], out_hbm.at[:, cols], sems.at[1, k])
            )
        for load in loads[:AHEAD]:
            load.start()
        for ref, side in ((own_ref, parity), (other_ref, 1 - parity)):
            for chip in range(chips):
                source = chip * CORES + side
                value = ref[chip]
                there = pl.ds(pl.multiple_of(source * latents, latents), latents)
                lhs[there, :] = jnp.where(source <= target, value, jnp.zeros_like(value))
        for k in range(steps):
            cols = pl.ds(offsets[k], COLUMNS[k])
            loads[k].wait()
            if k + AHEAD < steps:
                loads[k + AHEAD].start()
            out_buf[:, cols] = jnp.dot(
                lhs[...], error_buf[:, cols], preferred_element_type=jnp.float32
            ).astype(jnp.bfloat16)
            stores[k].start()
        for store in stores:
            store.wait()

    return pl.pallas_call(
        kernel,
        out_shape=jax.ShapeDtypeStruct((rows, width), jnp.bfloat16),
        in_specs=[SMEM, HBM, VMEM, VMEM],
        out_specs=HBM,
        scratch_shapes=[
            pltpu.VMEM((rows, tokens), jnp.bfloat16),
            pltpu.VMEM((tokens, width), jnp.bfloat16),
            pltpu.VMEM((rows, width), jnp.bfloat16),
            pltpu.SemaphoreType.DMA((2, steps)),
        ],
        compiler_params=params(28),
        cost_estimate=pl.CostEstimate(
            flops=2 * rows * tokens * width, transcendentals=0,
            bytes_accessed=2 * (rows + tokens) * width,
        ),
        name="decoder",
    )(place, errors, own, other)


def encoder(parts, mask, inputs):
    tokens, width = inputs.shape
    chips = parts.shape[0]
    latents = mask.shape[0]
    columns = 1024
    steps = width // columns

    def kernel(parts_ref, mask_ref, input_hbm, code_ref, out_ref, buf, sems):
        loads = []
        for k in range(steps):
            cols = pl.ds(k * columns, columns)
            loads.append(pltpu.make_async_copy(input_hbm.at[:, cols], buf.at[k], sems.at[k]))
        for load in loads[:AHEAD]:
            load.start()
        total = parts_ref[0].astype(jnp.float32)
        for chip in range(1, chips):
            total = total + parts_ref[chip].astype(jnp.float32)
        total = total.T
        code = jnp.concatenate([total[:latents], total[latents:]], axis=1)
        code_ref[...] = code
        pre = (code * mask_ref[...].astype(jnp.float32)).astype(jnp.bfloat16)
        for k in range(steps):
            loads[k].wait()
            if k + AHEAD < steps:
                loads[k + AHEAD].start()
            out_ref[:, pl.ds(k * columns, columns)] = jnp.dot(
                pre, buf[k], preferred_element_type=jnp.float32
            ).astype(jnp.bfloat16)

    return pl.pallas_call(
        kernel,
        out_shape=[
            jax.ShapeDtypeStruct((latents, tokens), jnp.float32),
            jax.ShapeDtypeStruct((latents, width), jnp.bfloat16),
        ],
        in_specs=[VMEM, VMEM, HBM],
        out_specs=[VMEM, VMEM],
        scratch_shapes=[
            pltpu.VMEM((steps, tokens, columns), jnp.bfloat16),
            pltpu.SemaphoreType.DMA((steps,)),
        ],
        compiler_params=params(16),
        name="encoder",
    )(parts, mask, inputs)


def step(saved_codes, relu_mask, errors, decoders, inputs):
    layers = lax.axis_size("layer")
    chips = layers // CORES
    target = lax.axis_index("layer")
    core = target % CORES
    latents, _ = saved_codes.shape[1:]
    hbm = lambda value: pltpu.with_memory_space_constraint(value, pltpu.HBM)
    target_error = hbm(errors[0])
    width = target_error.shape[1]
    swap = [(i, i ^ 1) for i in range(layers)]
    same_core = [[chip * CORES + c for chip in range(chips)] for c in range(CORES)]
    place_own = jnp.stack([core, target]).astype(jnp.int32)
    place_other = jnp.stack([1 - core, target]).astype(jnp.int32)

    def exchange(value):
        return lax.all_to_all(value, "layer", 0, 0, tiled=True, axis_index_groups=same_core)

    slabs = hbm(decoders[0].reshape(chips, CORES, latents, width))
    copies = gate(hbm(saved_codes[0]), hbm(relu_mask[0]), chips)
    mine = exchange(copies)
    away = code_terms(place_other, slabs, target_error, True)
    away = lax.ppermute(away, "layer", swap)
    own = code_terms(place_own, slabs, target_error, False)
    own, away = lax.optimization_barrier((own, away))
    terms = join(own, away, chips)
    terms, mine = lax.optimization_barrier((terms, mine))
    other = lax.ppermute(mine, "layer", swap)
    parts = exchange(terms)
    grads = decoder(place_own, mine, other, target_error)

    parts, grads = lax.optimization_barrier((parts, grads))
    code_grad, encoder_grad = encoder(parts, relu_mask[0], hbm(inputs[0]))
    return grads.reshape(1, layers, latents, width), code_grad[None], encoder_grad[None]


def solution(mesh):
    return jax.shard_map(
        step,
        mesh=mesh,
        in_specs=(
            P("layer", "lat", None),
            P("layer", "lat", None),
            P("layer", None, None),
            P("layer", None, "lat", None),
            P("layer", None, None),
        ),
        out_specs=(P("layer", None, "lat", None), P("layer", "lat", None), P("layer", "lat", None)),
        check_vma=False,
    )
```

```python
import jax
import jax.numpy as jnp
from jax import lax
from jax.experimental import pallas as pl
from jax.experimental.pallas import tpu as pltpu
from jax.sharding import PartitionSpec as P


CORES = 2
AHEAD = 2
HELD = 1024
DEPTHS = (HELD, 1024, 1024, 1024)
COLUMNS = (512, 1536, 1536, 512)
FIRST = 512
REST = (1024, 1280, 1280)

HBM = pl.BlockSpec(memory_space=pltpu.HBM)
VMEM = pl.BlockSpec(memory_space=pltpu.VMEM)
SMEM = pl.BlockSpec(memory_space=pltpu.SMEM)


def params(mib):
    return pltpu.CompilerParams(vmem_limit_bytes=mib << 20)


def starts(sizes):
    return [sum(sizes[:i]) for i in range(len(sizes))]


def gate(place, slabs, errors, codes, mask):
    latents, tokens = codes.shape
    chips = slabs.shape[0]

    def kernel(
        place_ref, slab_hbm, error_hbm, codes_hbm, mask_hbm, out_hbm, error_ref, slab_ref,
        buf, mask_buf, sems,
    ):
        cols = pl.ds(0, HELD)
        loads = [
            pltpu.make_async_copy(codes_hbm, buf, sems.at[chips]),
            pltpu.make_async_copy(mask_hbm, mask_buf, sems.at[chips + 1]),
        ]
        held = [
            pltpu.make_async_copy(
                slab_hbm.at[:, place_ref[0], :, cols], slab_ref, sems.at[chips + 2]
            ),
            pltpu.make_async_copy(error_hbm.at[:, cols], error_ref, sems.at[chips + 3]),
        ]
        copies = [
            pltpu.make_async_copy(buf, out_hbm.at[chip], sems.at[chip]) for chip in range(chips)
        ]
        for load in loads + held:
            load.start()
        for load in loads:
            load.wait()
        buf[...] = buf[...] * mask_buf[...].astype(jnp.bfloat16)
        for copy in copies:
            copy.start()
        for copy in copies + held:
            copy.wait()

    return pl.pallas_call(
        kernel,
        out_shape=[
            pltpu.HBM((chips, latents, tokens), jnp.bfloat16),
            jax.ShapeDtypeStruct((tokens, HELD), jnp.bfloat16),
            jax.ShapeDtypeStruct((chips, latents, HELD), jnp.bfloat16),
        ],
        in_specs=[SMEM, HBM, HBM, HBM, HBM],
        out_specs=[HBM, VMEM, VMEM],
        scratch_shapes=[
            pltpu.VMEM((latents, tokens), jnp.bfloat16),
            pltpu.VMEM((latents, tokens), jnp.int32),
            pltpu.SemaphoreType.DMA((chips + 4,)),
        ],
        compiler_params=params(8),
        name="gate",
    )(place, slabs, errors, codes, mask)


def code_terms(place, slabs, errors, *held, inputs=None):
    chips, _, latents, width = slabs.shape
    tokens = errors.shape[0]
    rows = chips * latents
    offsets = starts(DEPTHS)
    steps = len(DEPTHS)

    def kernel(place_ref, slab_hbm, error_hbm, *refs):
        held_refs = refs[: len(held)]
        slab_buf, error_buf, sems = refs[-3:]
        out = refs[-4]
        if inputs is not None:
            input_hbm, first_ref, out = refs[len(held) : len(held) + 3]
            first = pltpu.make_async_copy(
                input_hbm.at[:, pl.ds(0, FIRST)], first_ref, sems.at[0, 0]
            )
        parity, target = place_ref[0], place_ref[1]
        loads = []
        for k in range(steps):
            cols = pl.ds(offsets[k], DEPTHS[k])
            group = []
            if k or not held:
                group.append(
                    pltpu.make_async_copy(
                        error_hbm.at[:, cols], error_buf.at[:, cols], sems.at[0, k]
                    )
                )
            if k or len(held) < 2:
                group.append(
                    pltpu.make_async_copy(
                        slab_hbm.at[:, parity, :, cols], slab_buf.at[:, :, cols], sems.at[1, k]
                    )
                )
            loads.append(group)
        for pair in loads[:AHEAD]:
            for load in pair:
                load.start()
        source = (lax.broadcasted_iota(jnp.int32, (1, rows), 1) // latents) * CORES + parity
        keep = (source <= target).astype(jnp.float32)
        for k in range(steps):
            cols = pl.ds(offsets[k], DEPTHS[k])
            for load in loads[k]:
                load.wait()
            if k + AHEAD < steps:
                for load in loads[k + AHEAD]:
                    load.start()
            error = held_refs[0][...] if k == 0 and held else error_buf[:, cols]
            slab = held_refs[1][...] if k == 0 and len(held) > 1 else slab_buf[:, :, cols]
            part = lax.dot_general(
                error, slab.reshape(rows, DEPTHS[k]),
                (((1,), (1,)), ((), ())), preferred_element_type=jnp.float32,
            )
            if k == 0:
                out[...] = part
            elif k < steps - 1:
                out[...] += part
            else:
                out[...] = (out[...] + part) * keep
            if inputs is not None and k == steps - 1 - AHEAD:
                first.start()
        if inputs is not None:
            first.wait()

    out_shape = [jax.ShapeDtypeStruct((tokens, rows), jnp.float32)]
    extra = ()
    if inputs is not None:
        out_shape = [jax.ShapeDtypeStruct((tokens, FIRST), jnp.bfloat16)] + out_shape
        extra = (inputs,)
    return pl.pallas_call(
        kernel,
        out_shape=out_shape,
        in_specs=[SMEM, HBM, HBM] + [VMEM] * len(held) + [HBM] * len(extra),
        out_specs=[VMEM] * len(out_shape),
        scratch_shapes=[
            pltpu.VMEM((chips, latents, width), jnp.bfloat16),
            pltpu.VMEM((tokens, width), jnp.bfloat16),
            pltpu.SemaphoreType.DMA((2, steps)),
        ],
        compiler_params=params(24),
        cost_estimate=pl.CostEstimate(
            flops=2 * rows * tokens * width, transcendentals=0,
            bytes_accessed=2 * (rows + tokens) * width,
        ),
    )(place, slabs, errors, *held, *extra)


def join(own, away, chips):
    tokens, rows = own.shape
    latents = rows // chips
    half, lanes = tokens // 2, CORES * latents
    pairs = rows // lanes

    def kernel(own_ref, away_ref, out_hbm, out_buf, sems):
        left = lax.broadcasted_iota(jnp.int32, (half, lanes), 1) < latents
        stores = []
        for pair in range(pairs):
            cols = pl.ds(pair * lanes, lanes)
            low = own_ref[pl.ds(0, half), cols] + away_ref[pl.ds(0, half), cols]
            high = own_ref[pl.ds(half, half), cols] + away_ref[pl.ds(half, half), cols]
            out_buf[2 * pair] = jnp.where(
                left, low, pltpu.roll(high, latents, axis=1)
            ).astype(jnp.bfloat16)
            out_buf[2 * pair + 1] = jnp.where(
                left, pltpu.roll(low, latents, axis=1), high
            ).astype(jnp.bfloat16)
            both = pl.ds(2 * pair, 2)
            store = pltpu.make_async_copy(out_buf.at[both], out_hbm.at[both], sems.at[pair])
            store.start()
            stores.append(store)
        for store in stores:
            store.wait()

    return pl.pallas_call(
        kernel,
        out_shape=jax.ShapeDtypeStruct((chips, half, lanes), jnp.bfloat16),
        in_specs=[VMEM, VMEM],
        out_specs=HBM,
        scratch_shapes=[
            pltpu.VMEM((chips, half, lanes), jnp.bfloat16),
            pltpu.SemaphoreType.DMA((pairs,)),
        ],
        compiler_params=params(8),
        name="join",
    )(own, away)


def decoder(place, own, other, errors):
    tokens, width = errors.shape
    chips, latents, _ = own.shape
    rows = chips * CORES * latents
    offsets = starts(COLUMNS)
    steps = len(COLUMNS)

    def kernel(
        place_ref, error_hbm, own_ref, other_ref, out_hbm, lhs, error_buf, out_buf, sems
    ):
        parity, target = place_ref[0], place_ref[1]
        loads, stores = [], []
        for k in range(steps):
            cols = pl.ds(offsets[k], COLUMNS[k])
            loads.append(
                pltpu.make_async_copy(error_hbm.at[:, cols], error_buf.at[:, cols], sems.at[0, k])
            )
            stores.append(
                pltpu.make_async_copy(out_buf.at[:, cols], out_hbm.at[:, cols], sems.at[1, k])
            )
        rows_in = [
            pltpu.make_async_copy(ref, lhs.at[:, side], sems.at[2, 1 + n])
            for n, (ref, side) in enumerate(((own_ref, parity), (other_ref, 1 - parity)))
        ]
        for copy in rows_in:
            copy.start()
        for load in loads[:AHEAD]:
            load.start()
        for copy in rows_in:
            copy.wait()
        for source in range(chips * CORES):
            @pl.when(source > target)
            def _(source=source):
                lhs[source // CORES, source % CORES] = jnp.zeros((latents, tokens), jnp.bfloat16)

        for k in range(steps):
            cols = pl.ds(offsets[k], COLUMNS[k])
            loads[k].wait()
            if k + AHEAD < steps:
                loads[k + AHEAD].start()
            out_buf[:, cols] = jnp.dot(
                lhs[...].reshape(rows, tokens), error_buf[:, cols], preferred_element_type=jnp.float32
            ).astype(jnp.bfloat16)
            stores[k].start()
        for store in stores:
            store.wait()

    return pl.pallas_call(
        kernel,
        out_shape=jax.ShapeDtypeStruct((rows, width), jnp.bfloat16),
        in_specs=[SMEM, HBM, HBM, HBM],
        out_specs=HBM,
        scratch_shapes=[
            pltpu.VMEM((chips, CORES, latents, tokens), jnp.bfloat16),
            pltpu.VMEM((tokens, width), jnp.bfloat16),
            pltpu.VMEM((rows, width), jnp.bfloat16),
            pltpu.SemaphoreType.DMA((3, steps)),
        ],
        compiler_params=params(28),
        cost_estimate=pl.CostEstimate(
            flops=2 * rows * tokens * width, transcendentals=0,
            bytes_accessed=2 * (rows + tokens) * width,
        ),
        name="decoder",
    )(place, errors, own, other)


def encoder(parts, mask, inputs, held):
    tokens, width = inputs.shape
    chips = parts.shape[0]
    latents = mask.shape[0]
    sizes = (FIRST, *REST)
    offsets = starts(sizes)
    steps = len(sizes)

    def kernel(
        parts_ref, mask_ref, input_hbm, held_ref, code_hbm, out_hbm, buf, code_buf, out_buf, sems
    ):
        loads, stores = [None], []
        for k in range(steps):
            cols = pl.ds(offsets[k], sizes[k])
            if k:
                loads.append(
                    pltpu.make_async_copy(input_hbm.at[:, cols], buf.at[:, cols], sems.at[0, k])
                )
                loads[k].start()
            stores.append(
                pltpu.make_async_copy(out_buf.at[:, cols], out_hbm.at[:, cols], sems.at[1, k])
            )
        total = parts_ref[0].astype(jnp.float32)
        for chip in range(1, chips):
            total = total + parts_ref[chip].astype(jnp.float32)
        total = total.T
        code = jnp.concatenate([total[:latents], total[latents:]], axis=1)
        code_buf[...] = code
        stores.append(pltpu.make_async_copy(code_buf, code_hbm, sems.at[0, 0]))
        stores[-1].start()
        pre = (code * mask_ref[...].astype(jnp.float32)).astype(jnp.bfloat16)
        for k in range(steps):
            cols = pl.ds(offsets[k], sizes[k])
            if k:
                loads[k].wait()
            out_buf[:, cols] = jnp.dot(
                pre, buf[:, cols] if k else held_ref[...], preferred_element_type=jnp.float32
            ).astype(jnp.bfloat16)
            stores[k].start()
        for store in stores:
            store.wait()

    return pl.pallas_call(
        kernel,
        out_shape=[
            pltpu.HBM((latents, tokens), jnp.float32),
            pltpu.HBM((latents, width), jnp.bfloat16),
        ],
        in_specs=[VMEM, VMEM, HBM, VMEM],
        out_specs=[HBM, HBM],
        scratch_shapes=[
            pltpu.VMEM((tokens, width), jnp.bfloat16),
            pltpu.VMEM((latents, tokens), jnp.float32),
            pltpu.VMEM((latents, width), jnp.bfloat16),
            pltpu.SemaphoreType.DMA((2, steps)),
        ],
        compiler_params=params(16),
        name="encoder",
    )(parts, mask, inputs, held)


def step(saved_codes, relu_mask, errors, decoders, inputs):
    layers = lax.axis_size("layer")
    chips = layers // CORES
    target = lax.axis_index("layer")
    core = target % CORES
    latents, _ = saved_codes.shape[1:]
    hbm = lambda value: pltpu.with_memory_space_constraint(value, pltpu.HBM)
    target_error, layer_inputs = hbm(errors[0]), hbm(inputs[0])
    width = target_error.shape[1]
    swap = [(i, i ^ 1) for i in range(layers)]
    same_core = [[chip * CORES + c for chip in range(chips)] for c in range(CORES)]
    place_own = jnp.stack([core, target]).astype(jnp.int32)
    place_other = jnp.stack([1 - core, target]).astype(jnp.int32)

    def exchange(value):
        return lax.all_to_all(value, "layer", 0, 0, tiled=True, axis_index_groups=same_core)

    slabs = hbm(decoders[0].reshape(chips, CORES, latents, width))
    copies, held_error, held_slab = gate(
        place_other, slabs, target_error, hbm(saved_codes[0]), hbm(relu_mask[0])
    )
    mine = exchange(copies)
    (away,) = code_terms(place_other, slabs, target_error, held_error, held_slab)
    away = lax.ppermute(away, "layer", swap)
    held_inputs, own = code_terms(place_own, slabs, target_error, held_error, inputs=layer_inputs)
    own, away = lax.optimization_barrier((own, away))
    terms = join(own, away, chips)
    terms, mine = lax.optimization_barrier((terms, mine))
    other = lax.ppermute(mine, "layer", swap)
    parts = exchange(terms)
    grads = decoder(place_own, hbm(mine), hbm(other), target_error)

    parts, grads = lax.optimization_barrier((parts, grads))
    code_grad, encoder_grad = encoder(
        parts, relu_mask[0], layer_inputs, held_inputs
    )
    return grads.reshape(1, layers, latents, width), code_grad[None], encoder_grad[None]


def solution(mesh):
    return jax.shard_map(
        step,
        mesh=mesh,
        in_specs=(
            P("layer", "lat", None),
            P("layer", "lat", None),
            P("layer", None, None),
            P("layer", None, "lat", None),
            P("layer", None, None),
        ),
        out_specs=(P("layer", None, "lat", None), P("layer", "lat", None), P("layer", "lat", None)),
        check_vma=False,
    )
```

```python
import jax
import jax.numpy as jnp
from jax import lax
from jax.experimental import pallas as pl
from jax.experimental.pallas import tpu as pltpu
from jax.sharding import PartitionSpec as P


CORES = 2
AHEAD = 2
HELD = 1024
DEPTHS = (HELD, 1024, 1024, 1024)
COLUMNS = (512, 1536, 1536, 512)
FIRST = 512
REST = (512,) * 7

HBM = pl.BlockSpec(memory_space=pltpu.HBM)
VMEM = pl.BlockSpec(memory_space=pltpu.VMEM)
SMEM = pl.BlockSpec(memory_space=pltpu.SMEM)


def params(mib):
    return pltpu.CompilerParams(vmem_limit_bytes=mib << 20)


def starts(sizes):
    return [sum(sizes[:i]) for i in range(len(sizes))]


def gate(place, slabs, errors, codes, mask):
    latents, tokens = codes.shape
    chips = slabs.shape[0]

    def kernel(
        place_ref, slab_hbm, error_hbm, codes_hbm, mask_hbm, out_hbm, error_ref, slab_ref,
        buf, mask_buf, sems,
    ):
        cols = pl.ds(0, HELD)
        loads = [
            pltpu.make_async_copy(codes_hbm, buf, sems.at[chips]),
            pltpu.make_async_copy(mask_hbm, mask_buf, sems.at[chips + 1]),
        ]
        held = [
            pltpu.make_async_copy(
                slab_hbm.at[:, place_ref[0], :, cols], slab_ref, sems.at[chips + 2]
            ),
            pltpu.make_async_copy(error_hbm.at[:, cols], error_ref, sems.at[chips + 3]),
        ]
        copies = [
            pltpu.make_async_copy(buf, out_hbm.at[chip], sems.at[chip]) for chip in range(chips)
        ]
        for load in loads + held:
            load.start()
        for load in loads:
            load.wait()
        buf[...] = buf[...] * mask_buf[...].astype(jnp.bfloat16)
        for copy in copies:
            copy.start()
        for copy in copies + held:
            copy.wait()

    return pl.pallas_call(
        kernel,
        out_shape=[
            pltpu.HBM((chips, latents, tokens), jnp.bfloat16),
            jax.ShapeDtypeStruct((tokens, HELD), jnp.bfloat16),
            jax.ShapeDtypeStruct((chips, latents, HELD), jnp.bfloat16),
        ],
        in_specs=[SMEM, HBM, HBM, HBM, HBM],
        out_specs=[HBM, VMEM, VMEM],
        scratch_shapes=[
            pltpu.VMEM((latents, tokens), jnp.bfloat16),
            pltpu.VMEM((latents, tokens), jnp.int32),
            pltpu.SemaphoreType.DMA((chips + 4,)),
        ],
        compiler_params=params(8),
        name="gate",
    )(place, slabs, errors, codes, mask)


def code_terms(place, slabs, errors, *held, inputs=None):
    chips, _, latents, width = slabs.shape
    tokens = errors.shape[0]
    rows = chips * latents
    offsets = starts(DEPTHS)
    steps = len(DEPTHS)

    def kernel(place_ref, slab_hbm, error_hbm, *refs):
        held_refs = refs[: len(held)]
        slab_buf, error_buf, sems = refs[-3:]
        if inputs is not None:
            input_hbm, first_ref, out = refs[len(held) : len(held) + 3]
            first = pltpu.make_async_copy(
                input_hbm.at[:, pl.ds(0, FIRST)], first_ref, sems.at[0, 0]
            )
        else:
            first_ref, out = refs[len(held) : len(held) + 2]
            first = pltpu.make_async_copy(
                slab_hbm.at[:, 1 - place_ref[0], :, pl.ds(0, HELD)], first_ref, sems.at[0, 0]
            )
        parity, target = place_ref[0], place_ref[1]
        loads = []
        for k in range(steps):
            cols = pl.ds(offsets[k], DEPTHS[k])
            group = []
            if k or not held:
                group.append(
                    pltpu.make_async_copy(
                        error_hbm.at[:, cols], error_buf.at[:, cols], sems.at[0, k]
                    )
                )
            if k or len(held) < 2:
                group.append(
                    pltpu.make_async_copy(
                        slab_hbm.at[:, parity, :, cols], slab_buf.at[:, :, cols], sems.at[1, k]
                    )
                )
            loads.append(group)
        for pair in loads[:AHEAD]:
            for load in pair:
                load.start()
        source = (lax.broadcasted_iota(jnp.int32, (1, rows), 1) // latents) * CORES + parity
        keep = (source <= target).astype(jnp.float32)
        for k in range(steps):
            cols = pl.ds(offsets[k], DEPTHS[k])
            for load in loads[k]:
                load.wait()
            if k + AHEAD < steps:
                for load in loads[k + AHEAD]:
                    load.start()
            error = held_refs[0][...] if k == 0 and held else error_buf[:, cols]
            slab = held_refs[1][...] if k == 0 and len(held) > 1 else slab_buf[:, :, cols]
            part = lax.dot_general(
                error, slab.reshape(rows, DEPTHS[k]),
                (((1,), (1,)), ((), ())), preferred_element_type=jnp.float32,
            )
            if k == 0:
                out[...] = part
            elif k < steps - 1:
                out[...] += part
            else:
                out[...] = (out[...] + part) * keep
            if k == steps - 1 - AHEAD:
                first.start()
        first.wait()

    out_shape = [
        jax.ShapeDtypeStruct((chips, latents, HELD), jnp.bfloat16)
        if inputs is None
        else jax.ShapeDtypeStruct((tokens, FIRST), jnp.bfloat16),
        jax.ShapeDtypeStruct((tokens, rows), jnp.float32),
    ]
    extra = () if inputs is None else (inputs,)
    return pl.pallas_call(
        kernel,
        out_shape=out_shape,
        in_specs=[SMEM, HBM, HBM] + [VMEM] * len(held) + [HBM] * len(extra),
        out_specs=[VMEM] * len(out_shape),
        scratch_shapes=[
            pltpu.VMEM((chips, latents, width), jnp.bfloat16),
            pltpu.VMEM((tokens, width), jnp.bfloat16),
            pltpu.SemaphoreType.DMA((2, steps)),
        ],
        compiler_params=params(24),
        cost_estimate=pl.CostEstimate(
            flops=2 * rows * tokens * width, transcendentals=0,
            bytes_accessed=2 * (rows + tokens) * width,
        ),
    )(place, slabs, errors, *held, *extra)


def join(own, away, chips):
    tokens, rows = own.shape
    latents = rows // chips
    half, lanes = tokens // 2, CORES * latents
    pairs = rows // lanes

    def kernel(own_ref, away_ref, out_hbm, out_buf, sems):
        left = lax.broadcasted_iota(jnp.int32, (half, lanes), 1) < latents
        stores = []
        for pair in range(pairs):
            cols = pl.ds(pair * lanes, lanes)
            low = own_ref[pl.ds(0, half), cols] + away_ref[pl.ds(0, half), cols]
            high = own_ref[pl.ds(half, half), cols] + away_ref[pl.ds(half, half), cols]
            out_buf[2 * pair] = jnp.where(
                left, low, pltpu.roll(high, latents, axis=1)
            ).astype(jnp.bfloat16)
            out_buf[2 * pair + 1] = jnp.where(
                left, pltpu.roll(low, latents, axis=1), high
            ).astype(jnp.bfloat16)
            both = pl.ds(2 * pair, 2)
            store = pltpu.make_async_copy(out_buf.at[both], out_hbm.at[both], sems.at[pair])
            store.start()
            stores.append(store)
        for store in stores:
            store.wait()

    return pl.pallas_call(
        kernel,
        out_shape=jax.ShapeDtypeStruct((chips, half, lanes), jnp.bfloat16),
        in_specs=[VMEM, VMEM],
        out_specs=HBM,
        scratch_shapes=[
            pltpu.VMEM((chips, half, lanes), jnp.bfloat16),
            pltpu.SemaphoreType.DMA((pairs,)),
        ],
        compiler_params=params(8),
        name="join",
    )(own, away)


def decoder(place, own, other, errors):
    tokens, width = errors.shape
    chips, latents, _ = own.shape
    rows = chips * CORES * latents
    offsets = starts(COLUMNS)
    steps = len(COLUMNS)

    def kernel(
        place_ref, error_hbm, own_ref, other_ref, out_hbm, lhs, error_buf, out_buf, sems
    ):
        parity, target = place_ref[0], place_ref[1]
        loads, stores = [], []
        for k in range(steps):
            cols = pl.ds(offsets[k], COLUMNS[k])
            loads.append(
                pltpu.make_async_copy(error_hbm.at[:, cols], error_buf.at[:, cols], sems.at[0, k])
            )
            stores.append(
                pltpu.make_async_copy(out_buf.at[:, cols], out_hbm.at[:, cols], sems.at[1, k])
            )
        rows_in = [
            pltpu.make_async_copy(ref, lhs.at[:, side], sems.at[2, 1 + n])
            for n, (ref, side) in enumerate(((own_ref, parity), (other_ref, 1 - parity)))
        ]
        for copy in rows_in:
            copy.start()
        for load in loads[:AHEAD]:
            load.start()
        for copy in rows_in:
            copy.wait()
        for source in range(chips * CORES):
            @pl.when(source > target)
            def _(source=source):
                lhs[source // CORES, source % CORES] = jnp.zeros((latents, tokens), jnp.bfloat16)

        for k in range(steps):
            cols = pl.ds(offsets[k], COLUMNS[k])
            loads[k].wait()
            if k + AHEAD < steps:
                loads[k + AHEAD].start()
            out_buf[:, cols] = jnp.dot(
                lhs[...].reshape(rows, tokens), error_buf[:, cols], preferred_element_type=jnp.float32
            ).astype(jnp.bfloat16)
            stores[k].start()
        for store in stores:
            store.wait()

    return pl.pallas_call(
        kernel,
        out_shape=jax.ShapeDtypeStruct((rows, width), jnp.bfloat16),
        in_specs=[SMEM, HBM, HBM, HBM],
        out_specs=HBM,
        scratch_shapes=[
            pltpu.VMEM((chips, CORES, latents, tokens), jnp.bfloat16),
            pltpu.VMEM((tokens, width), jnp.bfloat16),
            pltpu.VMEM((rows, width), jnp.bfloat16),
            pltpu.SemaphoreType.DMA((3, steps)),
        ],
        compiler_params=params(28),
        cost_estimate=pl.CostEstimate(
            flops=2 * rows * tokens * width, transcendentals=0,
            bytes_accessed=2 * (rows + tokens) * width,
        ),
        name="decoder",
    )(place, errors, own, other)


def encoder(parts, mask, inputs, held):
    tokens, width = inputs.shape
    chips = parts.shape[0]
    latents = mask.shape[0]
    sizes = (FIRST, *REST)
    offsets = starts(sizes)
    steps = len(sizes)

    def kernel(
        parts_ref, mask_ref, input_hbm, held_ref, code_hbm, out_hbm, buf, code_buf, out_buf, sems
    ):
        loads, stores = [None], []
        for k in range(steps):
            cols = pl.ds(offsets[k], sizes[k])
            if k:
                loads.append(
                    pltpu.make_async_copy(input_hbm.at[:, cols], buf.at[:, cols], sems.at[0, k])
                )
                loads[k].start()
            stores.append(
                pltpu.make_async_copy(out_buf.at[:, cols], out_hbm.at[:, cols], sems.at[1, k])
            )
        total = parts_ref[0].astype(jnp.float32)
        for chip in range(1, chips):
            total = total + parts_ref[chip].astype(jnp.float32)
        total = total.T
        code = jnp.concatenate([total[:latents], total[latents:]], axis=1)
        code_buf[...] = code
        stores.append(pltpu.make_async_copy(code_buf, code_hbm, sems.at[0, 0]))
        stores[-1].start()
        pre = (code * mask_ref[...].astype(jnp.float32)).astype(jnp.bfloat16)
        for k in range(steps):
            cols = pl.ds(offsets[k], sizes[k])
            if k:
                loads[k].wait()
            out_buf[:, cols] = jnp.dot(
                pre, buf[:, cols] if k else held_ref[...], preferred_element_type=jnp.float32
            ).astype(jnp.bfloat16)
            stores[k].start()
        for store in stores:
            store.wait()

    return pl.pallas_call(
        kernel,
        out_shape=[
            pltpu.HBM((latents, tokens), jnp.float32),
            pltpu.HBM((latents, width), jnp.bfloat16),
        ],
        in_specs=[VMEM, VMEM, HBM, VMEM],
        out_specs=[HBM, HBM],
        scratch_shapes=[
            pltpu.VMEM((tokens, width), jnp.bfloat16),
            pltpu.VMEM((latents, tokens), jnp.float32),
            pltpu.VMEM((latents, width), jnp.bfloat16),
            pltpu.SemaphoreType.DMA((2, steps)),
        ],
        compiler_params=params(16),
        name="encoder",
    )(parts, mask, inputs, held)


def step(saved_codes, relu_mask, errors, decoders, inputs):
    layers = lax.axis_size("layer")
    chips = layers // CORES
    target = lax.axis_index("layer")
    core = target % CORES
    latents, _ = saved_codes.shape[1:]
    hbm = lambda value: pltpu.with_memory_space_constraint(value, pltpu.HBM)
    target_error, layer_inputs = hbm(errors[0]), hbm(inputs[0])
    width = target_error.shape[1]
    swap = [(i, i ^ 1) for i in range(layers)]
    same_core = [[chip * CORES + c for chip in range(chips)] for c in range(CORES)]
    place_own = jnp.stack([core, target]).astype(jnp.int32)
    place_other = jnp.stack([1 - core, target]).astype(jnp.int32)

    def exchange(value):
        return lax.all_to_all(value, "layer", 0, 0, tiled=True, axis_index_groups=same_core)

    slabs = hbm(decoders[0].reshape(chips, CORES, latents, width))
    copies, held_error, held_slab = gate(
        place_other, slabs, target_error, hbm(saved_codes[0]), hbm(relu_mask[0])
    )
    mine = exchange(copies)
    next_slab, away = code_terms(place_other, slabs, target_error, held_error, held_slab)
    away = lax.ppermute(away, "layer", swap)
    held_inputs, own = code_terms(
        place_own, slabs, target_error, held_error, next_slab, inputs=layer_inputs
    )
    own, away = lax.optimization_barrier((own, away))
    terms = join(own, away, chips)
    terms, mine = lax.optimization_barrier((terms, mine))
    other = lax.ppermute(mine, "layer", swap)
    parts = exchange(terms)
    grads = decoder(place_own, hbm(mine), hbm(other), target_error)

    parts, grads = lax.optimization_barrier((parts, grads))
    code_grad, encoder_grad = encoder(
        parts, relu_mask[0], layer_inputs, held_inputs
    )
    return grads.reshape(1, layers, latents, width), code_grad[None], encoder_grad[None]


def solution(mesh):
    return jax.shard_map(
        step,
        mesh=mesh,
        in_specs=(
            P("layer", "lat", None),
            P("layer", "lat", None),
            P("layer", None, None),
            P("layer", None, "lat", None),
            P("layer", None, None),
        ),
        out_specs=(P("layer", None, "lat", None), P("layer", "lat", None), P("layer", "lat", None)),
        check_vma=False,
    )
```
